32 devices in a mesh: blk: 8 (over y, x, core), feat: 4 (over z).
Axes of the slice: x: 2, y: 2, z: 4, core: 2. Of those that a mesh axis runs over, the one named last changes fastest.
Arguments:
- features: bfloat16 [128, 8192], P('feat', 'blk'), may hold values from -6 to 6
- weight_in: bfloat16 [128, 256], replicated, may hold values from -0.5 to 0.5
- weight_mid: bfloat16 [256, 256], replicated, may hold values from -0.375 to 0.375
- weight_out: bfloat16 [256, 172], replicated, may hold values from -0.375 to 0.375
- block_values: bfloat16 [8, 8, 16, 128, 128], P('blk'), may hold values from -0.25 to 0.25
- block_dst: int32 [8, 8, 16], P('blk'), may hold values from 0 to 7
- block_src: int32 [8, 8, 16], P('blk'), may hold values from 0 to 7
- block_count: int32 [8, 8], P('blk'), may hold values from 4 to 16, as said below
- labels: int32 [8192], P('blk'), may hold values from 0 to 171
- train_mask: int32 [8192], P('blk'), may hold values from 0 to 1
Outputs:
- loss: float32 [], replicated
- grad_in: float32 [128, 256], P('feat')
- grad_mid: float32 [256, 256], P('feat')
- grad_out: float32 [256, 172], P('feat')
The draws below stay inside these ranges and needn't reach their ends.
Inputs may be any that keep to these rules, and one draw needn't show every extreme that they name: block_count[b, p] is the number of live slots of the blocks of panel b's rows that read panel p's nodes; block_count[b, b] = 16. Entries of block_dst, block_src and block_values at slots at or past block_count are unused.
All inputs are finite; a program needn't handle non-finite values.
Results may differ from the reference program's by a relative error of at most 0.017.
Values may be sent and summed in bfloat16 or wider, within the bound.
A program may use at most 64 MiB of HBM per device.

```python
import jax
import jax.numpy as jnp
from jax import lax

F_IN = 128
HID = 256
CLASSES = 172
BLKSZ = 128
ROWBLK = 8
SLOTS = 16
PANELS = 8
PANEL = 1024
NODES = 8192


def draw_block_count(key, part):
    heavy_key, base_key = jax.random.split(key)
    heavy_rows = jax.random.randint(heavy_key, (PANELS, 1), 0, 4) == 3
    least = max(SLOTS // 4, 1)
    base_counts = jax.random.randint(base_key, (PANELS, PANELS), least, SLOTS // 2 + 1)
    counts = jnp.where(heavy_rows, SLOTS, base_counts)
    diagonal = jnp.arange(PANELS)[:, None] == jnp.arange(PANELS)[None, :]
    return jnp.where(diagonal, SLOTS, counts).astype(jnp.int32)


def draw_train_mask(key, part):
    panel_of = jnp.arange(NODES, dtype=jnp.int32) // PANEL
    uniform_draw = jax.random.randint(key, (NODES,), 0, 4 * PANELS)
    return (uniform_draw < PANELS + 2 * panel_of).astype(jnp.int32)


def plant(array, rng, low, largest):
    place = [jax.random.randint(jax.random.fold_in(rng, axis), (), 0, length) for axis, length in enumerate(array.shape)]
    main_axis = array.shape.index(max(array.shape))
    neighbour = place[:main_axis] + [(place[main_axis] + 1) % array.shape[main_axis]] + place[main_axis + 1:]
    return array.at[tuple(place)].set(low).at[tuple(neighbour)].set(largest)


def steps_of(rng, shape, shards, low, high):
    factor_of, own = 1.0, jax.random.fold_in(rng, 6)
    for axis_at, blocks in shards:
        draws = jnp.exp(jax.random.uniform(jax.random.fold_in(own, axis_at), (blocks,), jnp.float32, low / len(shards), high / len(shards)))
        factor_of = factor_of * jnp.repeat(draws, shape[axis_at] // blocks).reshape([-1 if axis == axis_at else 1 for axis in range(len(shape))])
    return factor_of


def bell_draw(key, extent, width, most, shards=(), held_as=jnp.bfloat16):
    drawn = jax.random.normal(key, extent, jnp.float32) * width
    if len(shards) > 0:
        drawn = steps_of(key, extent, shards, -0.22, 0.18) * drawn
    return jnp.clip(drawn, min=-most, max=most).astype(held_as)


def setup_inputs(seed: int = 0) -> dict:
    streams_of = jax.random.split(jax.random.key(seed), 11)
    return {
        "features": bell_draw(streams_of[0], (F_IN, NODES), 1.0, 6.0, ((0, 4), (1, 8))),
        "weight_in": bell_draw(streams_of[1], (F_IN, HID), F_IN ** -0.5, 0.5),
        "weight_mid": bell_draw(streams_of[2], (HID, HID), HID ** -0.5, 0.375),
        "weight_out": bell_draw(streams_of[3], (HID, CLASSES), HID ** -0.5, 0.375),
        "block_values": bell_draw(streams_of[4], (PANELS, PANELS, SLOTS, BLKSZ, BLKSZ), (4 * BLKSZ) ** -0.5, 0.25, ((0, 8),)),
        "block_dst": plant(jax.random.randint(streams_of[5], (PANELS, PANELS, SLOTS), 0, ROWBLK), jax.random.fold_in(streams_of[5], 1), 0, ROWBLK - 1).astype(jnp.int32),
        "block_src": plant(jax.random.randint(streams_of[6], (PANELS, PANELS, SLOTS), 0, ROWBLK), jax.random.fold_in(streams_of[6], 1), 0, ROWBLK - 1).astype(jnp.int32),
        "block_count": draw_block_count(jax.random.fold_in(streams_of[10], 71), 0),
        "labels": plant(jax.random.randint(streams_of[8], (NODES,), 0, CLASSES), jax.random.fold_in(streams_of[8], 1), 0, CLASSES - 1).astype(jnp.int32),
        "train_mask": draw_train_mask(jax.random.fold_in(streams_of[10], 71), 0),
    }


def aggregate(table, block_values, block_dst, block_src, block_count):
    breadth = table.shape[1]
    tiles = table.reshape(PANELS, ROWBLK, BLKSZ, breadth)
    slot_index = jnp.arange(SLOTS, dtype=jnp.int32)
    panel_index = jnp.arange(PANELS, dtype=jnp.int32)

    def one_panel(target_panel):
        values = block_values[target_panel].astype(jnp.float32)
        chosen = tiles[panel_index[:, None], block_src[target_panel]]
        live_slots = (slot_index[None, :] < block_count[target_panel][:, None]).astype(jnp.float32)
        product = jnp.einsum('psij,psjf->psif', values, chosen, precision=lax.Precision.HIGHEST)
        product = product * live_slots[:, :, None, None]
        empty = jnp.zeros((ROWBLK, BLKSZ, breadth), jnp.float32)
        return empty.at[block_dst[target_panel]].add(product)
    return lax.map(one_panel, panel_index).reshape(PANELS * ROWBLK * BLKSZ, breadth)

def elu(values):
    return jnp.where(values > 0, values, jnp.expm1(values))

def elu_slope(values):
    return jnp.where(values > 0, 1.0, jnp.exp(values))

def reference(features, weight_in, weight_mid, weight_out, block_values, block_dst, block_src, block_count, labels, train_mask):

    def spread(table):
        return aggregate(table, block_values, block_dst, block_src, block_count)
    first_agg = spread(features.T.astype(jnp.float32)).astype(jnp.bfloat16)
    first_pre = jnp.dot(first_agg, weight_in, preferred_element_type=jnp.float32)
    first_act = elu(first_pre).astype(jnp.bfloat16)
    second_agg = spread(first_act.astype(jnp.float32)).astype(jnp.bfloat16)
    second_pre = jnp.dot(second_agg, weight_mid, preferred_element_type=jnp.float32)
    second_act = elu(second_pre).astype(jnp.bfloat16)
    third_agg = spread(second_act.astype(jnp.float32)).astype(jnp.bfloat16)
    logits = jnp.dot(third_agg, weight_out, preferred_element_type=jnp.float32)
    log_total = jnp.log(lax.optimization_barrier(jnp.sum(jnp.exp(logits), axis=1)))
    one_hot = (labels[:, None] == jnp.arange(CLASSES, dtype=jnp.int32)[None, :]).astype(jnp.float32)
    picked = lax.optimization_barrier(jnp.sum(one_hot * logits, axis=1))
    weighting = train_mask.astype(jnp.float32)
    node_count = jnp.sum(weighting)
    loss = jnp.sum(weighting * (log_total - picked)) / jnp.maximum(node_count, 1.0)
    grad_logits = (weighting[:, None] * (jnp.exp(logits - log_total[:, None]) - one_hot)).astype(jnp.bfloat16)
    grad_out = jnp.dot(third_agg.T, grad_logits, preferred_element_type=jnp.float32)
    third_back = jnp.dot(grad_logits, weight_out.T, preferred_element_type=jnp.float32).astype(jnp.bfloat16)
    unused, transpose = jax.vjp(spread, jnp.zeros((NODES, HID), jnp.float32))
    second_grad = transpose(third_back.astype(jnp.float32))[0]
    second_gate = (second_grad * elu_slope(second_pre)).astype(jnp.bfloat16)
    grad_mid = jnp.dot(second_agg.T, second_gate, preferred_element_type=jnp.float32)
    second_back = jnp.dot(second_gate, weight_mid.T, preferred_element_type=jnp.float32).astype(jnp.bfloat16)
    first_grad = transpose(second_back.astype(jnp.float32))[0]
    first_gate = (first_grad * elu_slope(first_pre)).astype(jnp.bfloat16)
    grad_in = jnp.dot(first_agg.T, first_gate, preferred_element_type=jnp.float32)
    return (loss, grad_in, grad_mid, grad_out)
```

```python
import functools

import jax
import jax.numpy as jnp
from jax import lax
from jax.experimental import pallas as pl
from jax.experimental.pallas import tpu as pltpu
from jax.sharding import PartitionSpec as P

MESH = pl.DeviceIdType.MESH
NT = (((1,), (1,)), ((), ()))
F32 = jnp.float32
BF16 = jnp.bfloat16


def dot(a, b):
    return jnp.dot(a, b, preferred_element_type=F32)


def dot_nt(a, b):
    return lax.dot_general(a, b, NT, preferred_element_type=F32)


def elu(v):
    return jnp.where(v > 0, v, jnp.exp(jnp.minimum(v, 0.0)) - 1.0)


def elu_slope(v):
    return jnp.where(v > 0, 1.0, jnp.exp(jnp.minimum(v, 0.0)))


class Line:
    def __init__(self, table, sems, nf):
        self.table, self.sems, self.nf = table, sems, nf
        self.f = lax.axis_index("feat")

    def right(self, k):
        return pltpu.make_async_remote_copy(
            src_ref=self.table.at[self.f - k],
            dst_ref=self.table.at[self.f - k],
            send_sem=self.sems.at[0, k],
            recv_sem=self.sems.at[1, k + 1],
            device_id={"feat": self.f + 1},
            device_id_type=MESH,
        )

    def left(self, k):
        return pltpu.make_async_remote_copy(
            src_ref=self.table.at[self.f + k],
            dst_ref=self.table.at[self.f + k],
            send_sem=self.sems.at[2, k],
            recv_sem=self.sems.at[3, k + 1],
            device_id={"feat": self.f - 1},
            device_id_type=MESH,
        )

    def arrived(self, sem, slot):
        pltpu.make_async_copy(self.table.at[slot], self.table.at[slot], sem).wait()

    def start(self):
        @pl.when(self.f < self.nf - 1)
        def _():
            self.right(0).start()

        @pl.when(self.f > 0)
        def _():
            self.left(0).start()

    def finish(self):
        f, nf = self.f, self.nf
        for k in range(1, nf):

            @pl.when(f >= k)
            def _():
                self.arrived(self.sems.at[1, k], f - k)

                @pl.when(f < nf - 1)
                def _():
                    self.right(k).start()

            @pl.when(f + k <= nf - 1)
            def _():
                self.arrived(self.sems.at[3, k], f + k)

                @pl.when(f > 0)
                def _():
                    self.left(k).start()

        for k in range(nf):

            @pl.when(jnp.logical_and(f >= k, f < nf - 1))
            def _():
                self.right(k).wait_send()

            @pl.when(jnp.logical_and(f + k <= nf - 1, f > 0))
            def _():
                self.left(k).wait_send()


def step_kernel(
    n, nf, classes, slots,
    features, w_in, w_mid, w_out, out_rows, mid_rows, values,
    dst, src, w_fwd, w_bwd, labels, mask,
    loss_out, gin_out, gmid_out, gout_out,
    tab1, tab2, tab3, line1, line2, line3, line4, line5,
    back, acc, prod, win1, acc1, prod1, pre1, pre2,
    out_p, recv_p, out_s, recv_s,
    go_mine, go_part, go_pair, go_recv,
    gm_mine, gm_part, gm_pair, gm_recv,
    gi_mine, gi_part, gi_pair, gi_recv,
    blk_sems, line_sems, rs_sems, sum_sems,
):
    me = lax.axis_index("blk")
    f = lax.axis_index("feat")
    chip = me // 2
    side = me % 2
    chips = n // 2
    partner = chip * 2 + (1 - side)
    rb_count = tab2.shape[1]
    blk = tab2.shape[3]

    def far(k):
        return lax.rem(chip + k, chips) * 2 + side

    barrier = pltpu.get_barrier_semaphore()
    pl.semaphore_signal(barrier, inc=1, device_id={"blk": partner}, device_id_type=MESH)
    for k in range(1, chips):
        pl.semaphore_signal(barrier, inc=1, device_id={"blk": far(k)}, device_id_type=MESH)
    for other in (lax.rem(f + 1, nf), lax.rem(f + nf - 1, nf)):
        pl.semaphore_signal(barrier, inc=1, device_id={"feat": other}, device_id_type=MESH)
    pl.semaphore_wait(barrier, chips + 2)

    def remote(source, target, send, recv, device):
        return pltpu.make_async_remote_copy(
            src_ref=source, dst_ref=target, send_sem=send, recv_sem=recv,
            device_id={"blk": device}, device_id_type=MESH,
        )

    def lanes(rb):
        return slice(rb * blk, (rb + 1) * blk)

    def combine(product, weights, panel, rb):
        total = None
        for s in range(slots):
            term = product[s] * weights[(panel * slots + s) * rb_count + rb]
            total = term if total is None else total + term
        return total

    def aggregate(table, phase, total, product, window):
        def to_far(k):
            return remote(table.at[me], table.at[me], blk_sems.at[phase, 0, k],
                          blk_sems.at[phase, 1, k], far(k))

        def to_partner(k):
            panel = lax.rem(chip - k + chips, chips) * 2 + side
            return remote(table.at[panel], table.at[panel], blk_sems.at[phase, 2, k],
                          blk_sems.at[phase, 3, k], partner)

        for k in range(1, chips):
            to_far(k).start()
        to_partner(0).start()
        total[...] = jnp.zeros_like(total)

        def turn(t, carry):
            k = t // 2
            h = t % 2
            base = lax.rem(chip - k + chips, chips) * 2

            @pl.when(jnp.logical_and(h == 0, k > 0))
            def _():
                to_far(k).wait_recv()
                to_partner(k).start()

            @pl.when(h == 1)
            def _():
                to_partner(k).wait_recv()

            panel = base + jnp.where(h == 0, side, 1 - side)
            window[...] = table[panel]
            for s in range(slots):
                chosen = window[src[panel * slots + s]]
                product[s] = dot_nt(chosen, values[panel, s])
            for rb in range(rb_count):
                total[rb] += combine(product, w_fwd, panel, rb)
            return carry

        lax.fori_loop(0, n, turn, 0)
        for k in range(1, chips):
            to_far(k).wait_send()
        for k in range(chips):
            to_partner(k).wait_send()

    def spread(phase, own):
        def to_partner(k):
            return remote(out_p.at[phase, k], recv_p.at[phase, k], rs_sems.at[phase, 0, k],
                          rs_sems.at[phase, 1, k], partner)

        def to_far(k):
            return remote(out_s.at[phase, k], recv_s.at[phase, k], rs_sems.at[phase, 2, k],
                          rs_sems.at[phase, 3, k], far(k))

        def turn(t, carry):
            k = lax.rem(t // 2 + 1, chips)
            h = t % 2
            panel = lax.rem(chip + k, chips) * 2 + jnp.where(h == 0, 1 - side, side)
            for s in range(slots):
                chosen = back[dst[panel * slots + s]]
                prod[s] = dot(chosen, values[panel, s])
            for rb in range(rb_count):
                own[rb] = combine(prod, w_bwd, panel, rb)

            @pl.when(h == 0)
            def _():
                out_p[phase, k] = own[...].astype(BF16)
                to_partner(k).start()

            @pl.when(h == 1)
            def _():
                to_partner(k).wait_recv()
                own[...] += recv_p[phase, k].astype(F32)

                @pl.when(k > 0)
                def _():
                    out_s[phase, k] = own[...].astype(BF16)
                    to_far(k).start()

            return carry

        lax.fori_loop(0, n, turn, 0)
        for k in range(1, chips):
            to_far(k).wait_recv()
            own[...] += recv_s[phase, k].astype(F32)
        for k in range(1, chips):
            to_far(k).wait_send()
        for k in range(chips):
            to_partner(k).wait_send()

    class Total:
        def __init__(self, index, mine, part, pair, recv):
            self.index, self.mine, self.part, self.pair, self.recv = index, mine, part, pair, recv

        def near(self):
            return remote(self.mine, self.part, sum_sems.at[self.index, 0, 0],
                          sum_sems.at[self.index, 1, 0], partner)

        def wide(self, k):
            return remote(self.pair, self.recv.at[chip], sum_sems.at[self.index, 0, k],
                          sum_sems.at[self.index, 1, k], far(k))

        def spread_pair(self):
            self.near().wait_recv()
            self.pair[...] = self.mine[...] + self.part[...]
            for k in range(1, chips):
                self.wide(k).start()

        def result(self):
            self.recv[chip] = self.pair[...]
            for k in range(1, chips):
                source = lax.rem(chip - k + chips, chips)
                remote(self.pair, self.recv.at[source], sum_sems.at[self.index, 0, k],
                       sum_sems.at[self.index, 1, k], far(k)).wait_recv()
            total = self.recv[0]
            for c in range(1, chips):
                total = total + self.recv[c]
            self.near().wait_send()
            for k in range(1, chips):
                self.wide(k).wait_send()
            return total

    for rb in range(rb_count):
        tab1[me, rb] = features[:, lanes(rb)]
    aggregate(tab1, 0, acc1, prod1, win1)
    for rb in range(rb_count):
        line1[f, :, lanes(rb)] = acc1[rb].astype(BF16)
    gather = Line(line1, line_sems.at[0], nf)
    gather.start()
    gather.finish()
    pre = dot(w_in[0], line1[0])
    for g in range(1, nf):
        pre += dot(w_in[g], line1[g])
    pre1[...] = pre
    act = elu(pre).astype(BF16)
    for rb in range(rb_count):
        tab2[me, rb] = act[:, lanes(rb)]

    aggregate(tab2, 1, acc, prod, back)
    for rb in range(rb_count):
        line2[f, :, lanes(rb)] = acc[rb].astype(BF16)
    gather = Line(line2, line_sems.at[1], nf)
    gather.start()
    gather.finish()
    hidden = nf * line2.shape[1]
    nodes = line2.shape[2]
    pre = dot(w_mid[...], line2[...].reshape(hidden, nodes))
    pre2[...] = pre
    act = elu(pre).astype(BF16)
    for rb in range(rb_count):
        tab3[me, rb] = act[:, lanes(rb)]

    aggregate(tab3, 2, acc, prod, back)
    for rb in range(rb_count):
        line3[f, :, lanes(rb)] = acc[rb].astype(BF16)
    gather = Line(line3, line_sems.at[2], nf)
    gather.start()
    gather.finish()
    logits = dot(w_out[...], line3[...].reshape(hidden, nodes))
    rows = lax.broadcasted_iota(jnp.int32, logits.shape, 0)
    real = rows < classes
    log_total = jnp.log(jnp.sum(jnp.where(real, jnp.exp(logits), 0.0), axis=0, keepdims=True))
    one_hot = jnp.where(rows == labels[...], 1.0, 0.0)
    picked = jnp.sum(one_hot * logits, axis=0, keepdims=True)
    weighting = mask[...].astype(F32)
    loss_part = jnp.sum(weighting * (log_total - picked))
    count_part = jnp.sum(weighting)
    grads = jnp.where(real, weighting * (jnp.exp(logits - log_total) - one_hot), 0.0).astype(BF16)
    third = dot(out_rows[...], grads).astype(BF16)
    for rb in range(rb_count):
        back[rb] = third[:, lanes(rb)]
    hp = line3.shape[1]
    go_mine[...] = jnp.zeros_like(go_mine)
    go_mine[0:hp, 0 : grads.shape[0]] = dot_nt(line3[f], grads)
    stat_rows = lax.broadcasted_iota(jnp.int32, (8, go_mine.shape[1]), 0)
    go_mine[hp : hp + 8, :] = jnp.where(stat_rows == 0, loss_part, count_part)
    go_sum = Total(0, go_mine, go_part, go_pair, go_recv)
    go_sum.near().start()

    spread(0, acc)
    go_sum.spread_pair()
    for rb in range(rb_count):
        line4[f, :, lanes(rb)] = (acc[rb] * elu_slope(pre2[:, lanes(rb)])).astype(BF16)
    gather = Line(line4, line_sems.at[3], nf)
    gather.start()
    gather.finish()
    gate = line4[...].reshape(hidden, nodes)
    second = dot(mid_rows[...], gate).astype(BF16)
    for rb in range(rb_count):
        back[rb] = second[:, lanes(rb)]
    gm_mine[...] = dot_nt(line2[f], gate)
    gm_sum = Total(1, gm_mine, gm_part, gm_pair, gm_recv)
    gm_sum.near().start()

    spread(1, acc)
    gm_sum.spread_pair()
    for rb in range(rb_count):
        line5[f, :, lanes(rb)] = (acc[rb] * elu_slope(pre1[:, lanes(rb)])).astype(BF16)
    gather = Line(line5, line_sems.at[4], nf)
    gather.start()
    gather.finish()
    gate = line5[...].reshape(hidden, nodes)
    gi_mine[...] = dot_nt(line1[f], gate)
    gi_sum = Total(2, gi_mine, gi_part, gi_pair, gi_recv)
    gi_sum.near().start()
    gi_sum.spread_pair()
    total = go_sum.result()
    gout_out[...] = total[0:hp, 0:classes]
    loss_out[...] = total[hp : hp + 1, 0:1] / jnp.maximum(total[hp + 1 : hp + 2, 0:1], 1.0)
    gmid_out[...] = gm_sum.result()
    gin_out[...] = gi_sum.result()


def round_up(value, step):
    return (value + step - 1) // step * step


def shards(
    features, weight_in, weight_mid, weight_out, block_values,
    block_dst, block_src, block_count, labels, train_mask,
):
    n = lax.axis_size("blk")
    nf = lax.axis_size("feat")
    f = lax.axis_index("feat")
    in_part, nodes = features.shape
    hidden, classes = weight_out.shape
    hp = hidden // nf
    slots, blk = block_values.shape[2], block_values.shape[-1]
    rb_count = nodes // blk
    padded = round_up(classes, 16)
    wide = round_up(classes, 128)
    chips = n // 2

    w_in = lax.dynamic_slice_in_dim(weight_in, f * hp, hp, 1).T
    w_in = w_in.reshape(hp, nf, in_part).transpose(1, 0, 2)
    w_mid = lax.dynamic_slice_in_dim(weight_mid, f * hp, hp, 1).T
    out_pad = jnp.pad(weight_out, ((0, 0), (0, padded - classes)))
    w_out = out_pad.T
    out_rows = lax.dynamic_slice_in_dim(out_pad, f * hp, hp, 0)
    mid_rows = lax.dynamic_slice_in_dim(weight_mid, f * hp, hp, 0)
    live = jnp.arange(slots, dtype=jnp.int32)[None, :] < block_count[0][:, None]
    blocks = jnp.arange(rb_count, dtype=jnp.int32)
    w_fwd = ((block_dst[0][:, :, None] == blocks) & live[:, :, None]).astype(F32).reshape(-1)
    w_bwd = ((block_src[0][:, :, None] == blocks) & live[:, :, None]).astype(F32).reshape(-1)

    vmem = pl.BlockSpec(memory_space=pltpu.VMEM)
    smem = pl.BlockSpec(memory_space=pltpu.SMEM)

    def sums(rows, width):
        return [pltpu.VMEM((rows, width), F32)] * 3 + [pltpu.VMEM((chips, rows, width), F32)]

    tab = pltpu.VMEM((n, rb_count, hp, blk), BF16)
    line = pltpu.VMEM((nf, hp, nodes), BF16)
    stage = pltpu.VMEM((2, chips, rb_count, hp, blk), BF16)
    loss, gin, gmid, gout = pl.pallas_call(
        functools.partial(step_kernel, n, nf, classes, slots),
        out_shape=(
            jax.ShapeDtypeStruct((1, 1), F32),
            jax.ShapeDtypeStruct((in_part, hidden), F32),
            jax.ShapeDtypeStruct((hp, hidden), F32),
            jax.ShapeDtypeStruct((hp, classes), F32),
        ),
        in_specs=[vmem] * 7 + [smem] * 4 + [vmem] * 2,
        out_specs=(vmem,) * 4,
        scratch_shapes=[
            pltpu.VMEM((n, rb_count, in_part, blk), BF16), tab, tab,
            pltpu.VMEM((nf, in_part, nodes), BF16), line, line, line, line,
            pltpu.VMEM((rb_count, hp, blk), BF16),
            pltpu.VMEM((rb_count, hp, blk), F32),
            pltpu.VMEM((slots, hp, blk), F32),
            pltpu.VMEM((rb_count, in_part, blk), BF16),
            pltpu.VMEM((rb_count, in_part, blk), F32),
            pltpu.VMEM((slots, in_part, blk), F32),
            pltpu.VMEM((hp, nodes), F32), pltpu.VMEM((hp, nodes), F32),
            stage, stage, stage, stage,
            *sums(hp + 8, wide), *sums(hp, hidden), *sums(in_part, hidden),
            pltpu.SemaphoreType.DMA((3, 4, chips)),
            pltpu.SemaphoreType.DMA((5, 4, nf + 1)),
            pltpu.SemaphoreType.DMA((2, 4, chips)),
            pltpu.SemaphoreType.DMA((3, 2, chips)),
        ],
        compiler_params=pltpu.CompilerParams(
            collective_id=0, has_side_effects=True, vmem_limit_bytes=56 * 1024 * 1024
        ),
        name="step",
    )(
        features, w_in, w_mid, w_out, out_rows, mid_rows, block_values[0],
        block_dst.reshape(-1), block_src.reshape(-1), w_fwd, w_bwd,
        labels.reshape(1, -1), train_mask.reshape(1, -1),
    )
    return loss.reshape(()), gin, gmid, gout


def solution(mesh):
    placed = (
        P("feat", "blk"), P(), P(), P(), P("blk", None, None, None, None),
        P("blk", None, None), P("blk", None, None), P("blk", None), P("blk"), P("blk"),
    )
    return jax.shard_map(
        shards,
        mesh=mesh,
        in_specs=placed,
        out_specs=(P(), P("feat", None), P("feat", None), P("feat", None)),
        check_vma=False,
    )
```

```python
import functools

import jax
import jax.numpy as jnp
from jax import lax
from jax.experimental import pallas as pl
from jax.experimental.pallas import tpu as pltpu
from jax.sharding import PartitionSpec as P

MESH = pl.DeviceIdType.MESH
NT = (((1,), (1,)), ((), ()))
F32 = jnp.float32
BF16 = jnp.bfloat16


def dot(a, b):
    return jnp.dot(a, b, preferred_element_type=F32)


def dot_nt(a, b):
    return lax.dot_general(a, b, NT, preferred_element_type=F32)


def elu(v):
    return jnp.where(v > 0, v, jnp.exp(jnp.minimum(v, 0.0)) - 1.0)


def elu_slope(v):
    return jnp.where(v > 0, 1.0, jnp.exp(jnp.minimum(v, 0.0)))


class Line:
    def __init__(self, table, sems, nf):
        self.table, self.sems, self.nf = table, sems, nf
        self.f = lax.axis_index("feat")

    def right(self, k):
        return pltpu.make_async_remote_copy(
            src_ref=self.table.at[self.f - k],
            dst_ref=self.table.at[self.f - k],
            send_sem=self.sems.at[0, k],
            recv_sem=self.sems.at[1, k + 1],
            device_id={"feat": self.f + 1},
            device_id_type=MESH,
        )

    def left(self, k):
        return pltpu.make_async_remote_copy(
            src_ref=self.table.at[self.f + k],
            dst_ref=self.table.at[self.f + k],
            send_sem=self.sems.at[2, k],
            recv_sem=self.sems.at[3, k + 1],
            device_id={"feat": self.f - 1},
            device_id_type=MESH,
        )

    def arrived(self, sem, slot):
        pltpu.make_async_copy(self.table.at[slot], self.table.at[slot], sem).wait()

    def start(self):
        @pl.when(self.f < self.nf - 1)
        def _():
            self.right(0).start()

        @pl.when(self.f > 0)
        def _():
            self.left(0).start()

    def finish(self):
        f, nf = self.f, self.nf
        for k in range(1, nf):

            @pl.when(f >= k)
            def _():
                self.arrived(self.sems.at[1, k], f - k)

                @pl.when(f < nf - 1)
                def _():
                    self.right(k).start()

            @pl.when(f + k <= nf - 1)
            def _():
                self.arrived(self.sems.at[3, k], f + k)

                @pl.when(f > 0)
                def _():
                    self.left(k).start()

    def drain(self):
        f, nf = self.f, self.nf
        for k in range(nf):

            @pl.when(jnp.logical_and(f >= k, f < nf - 1))
            def _():
                self.right(k).wait_send()

            @pl.when(jnp.logical_and(f + k <= nf - 1, f > 0))
            def _():
                self.left(k).wait_send()


def step_kernel(
    n, nf, chunks, slots,
    features, w_in, w_mid, w_out, values, dst, src, count, labels, mask,
    loss_out, gin_out, gmid_out, gout_out,
    tab1, tab2, tab3, line1, line2, line3, line4,
    back, acc, prod, win1, acc1, prod1, pre1, pre2, w_in_t, w_mid_t, gate1,
    out_p, recv_p, out_s, recv_s,
    go_mine, go_part, go_pair, go_recv,
    gm_mine, gm_part, gm_pair, gm_recv,
    gi_mine, gi_part, gi_pair, gi_recv, gi_own, gi_swap,
    blk_sems, line_sems, rs_sems, sum_sems, swap_sems,
):
    me = lax.axis_index("blk")
    f = lax.axis_index("feat")
    chip = me // 2
    side = me % 2
    chips = n // 2
    partner = chip * 2 + (1 - side)
    rb_count = tab2.shape[1]
    blk = tab2.shape[3]
    in_part = features.shape[0]
    hp = tab2.shape[2]
    hidden = nf * hp
    part = rb_count // chunks
    classes = w_out.shape[1]

    def far(k):
        return lax.rem(chip + k, chips) * 2 + side

    barrier = pltpu.get_barrier_semaphore()
    pl.semaphore_signal(barrier, inc=1, device_id={"blk": partner}, device_id_type=MESH)
    for k in range(1, chips):
        pl.semaphore_signal(barrier, inc=1, device_id={"blk": far(k)}, device_id_type=MESH)
    for k in range(1, nf):
        pl.semaphore_signal(
            barrier, inc=1, device_id={"feat": lax.rem(f + k, nf)}, device_id_type=MESH
        )
    pl.semaphore_wait(barrier, chips + nf - 1)

    def remote(source, target, send, recv, device):
        return pltpu.make_async_remote_copy(
            src_ref=source, dst_ref=target, send_sem=send, recv_sem=recv,
            device_id={"blk": device}, device_id_type=MESH,
        )

    def lanes(rb):
        return slice(rb * blk, (rb + 1) * blk)

    def own_rows(ref):
        return ref[pl.ds(pl.multiple_of(f * hp, hp), hp), :]

    def combined(product, target, index, panel, add):
        live = count[0, panel]
        places = [jnp.where(s < live, index[0, panel, s], -1) for s in range(slots)]
        for rb in range(rb_count):
            total = target[rb] if add else None
            for s in range(slots):
                term = product[s] * jnp.where(places[s] == rb, 1.0, 0.0)
                total = term if total is None else total + term
            target[rb] = total

    def piece(table, panel, c):
        return table.at[panel, pl.ds(c * part, part)]

    class Gather:
        def __init__(self, table, phase):
            self.table, self.phase = table, phase

        def to_far(self, k, c):
            return remote(piece(self.table, me, c), piece(self.table, me, c),
                          blk_sems.at[self.phase, 0, k, c],
                          blk_sems.at[self.phase, 1, k, c], far(k))

        def to_partner(self, k, c):
            panel = lax.rem(chip - k + chips, chips) * 2 + side
            return remote(piece(self.table, panel, c), piece(self.table, panel, c),
                          blk_sems.at[self.phase, 2, k, c],
                          blk_sems.at[self.phase, 3, k, c], partner)

        def start(self, c):
            for k in range(1, chips):
                self.to_far(k, c).start()
            self.to_partner(0, c).start()

        def aggregate(self, total, product, window):
            total[...] = jnp.zeros_like(total)

            def turn(t, carry):
                k = t // 2
                h = t % 2
                base = lax.rem(chip - k + chips, chips) * 2

                @pl.when(jnp.logical_and(h == 0, k > 0))
                def _():
                    for c in range(chunks):
                        self.to_far(k, c).wait_recv()
                        self.to_partner(k, c).start()

                @pl.when(h == 1)
                def _():
                    for c in range(chunks):
                        self.to_partner(k, c).wait_recv()

                panel = base + jnp.where(h == 0, side, 1 - side)
                window[...] = self.table[panel]
                for s in range(slots):
                    chosen = window[src[0, panel, s]]
                    product[s] = dot_nt(chosen, values[0, panel, s])
                combined(product, total, dst, panel, True)
                return carry

            lax.fori_loop(0, n, turn, 0)
            for c in range(chunks):
                for k in range(1, chips):
                    self.to_far(k, c).wait_send()
                for k in range(chips):
                    self.to_partner(k, c).wait_send()

    def spread(phase, own, ready):
        def to_partner(k):
            return remote(out_p.at[phase, k], recv_p.at[phase, k], rs_sems.at[phase, 0, k, 0],
                          rs_sems.at[phase, 1, k, 0], partner)

        def to_far(k, c):
            rows = pl.ds(c * part, part)
            return remote(out_s.at[phase, k, rows], recv_s.at[phase, k, rows],
                          rs_sems.at[phase, 2, k, c], rs_sems.at[phase, 3, k, c], far(k))

        def turn(t, carry):
            k = lax.rem(t // 2 + 1, chips)
            h = t % 2
            panel = lax.rem(chip + k, chips) * 2 + jnp.where(h == 0, 1 - side, side)
            for s in range(slots):
                chosen = back[dst[0, panel, s]]
                prod[s] = dot(chosen, values[0, panel, s])
            combined(prod, own, src, panel, False)

            @pl.when(h == 0)
            def _():
                out_p[phase, k] = own[...].astype(BF16)
                to_partner(k).start()

            @pl.when(h == 1)
            def _():
                to_partner(k).wait_recv()
                own[...] += recv_p[phase, k].astype(F32)

                @pl.when(k > 0)
                def _():
                    out_s[phase, k] = own[...].astype(BF16)
                    to_far(k, 0).start()

            return carry

        lax.fori_loop(0, n, turn, 0)
        for c in range(1, chunks):
            for k in range(1, chips):
                to_far(k, c).start()
        for c in range(chunks):
            for k in range(1, chips):
                to_far(k, c).wait_recv()
            for rb in range(c * part, (c + 1) * part):
                total = own[rb]
                for k in range(1, chips):
                    total = total + recv_s[phase, k, rb].astype(F32)
                ready(c, rb, total)
            ready(c, None, None)
        for c in range(chunks):
            for k in range(1, chips):
                to_far(k, c).wait_send()
        for k in range(chips):
            to_partner(k).wait_send()

    class Total:
        def __init__(self, index, mine, part, pair, recv):
            self.index, self.mine, self.part, self.pair, self.recv = index, mine, part, pair, recv

        def near(self):
            return remote(self.mine, self.part, sum_sems.at[self.index, 0, 0],
                          sum_sems.at[self.index, 1, 0], partner)

        def wide(self, k):
            return remote(self.pair, self.recv.at[chip], sum_sems.at[self.index, 0, k],
                          sum_sems.at[self.index, 1, k], far(k))

        def spread_pair(self):
            self.near().wait_recv()
            self.pair[...] = self.mine[...] + self.part[...]
            for k in range(1, chips):
                self.wide(k).start()

        def result(self):
            self.recv[chip] = self.pair[...]
            for k in range(1, chips):
                source = lax.rem(chip - k + chips, chips)
                remote(self.pair, self.recv.at[source], sum_sems.at[self.index, 0, k],
                       sum_sems.at[self.index, 1, k], far(k)).wait_recv()
            total = self.recv[0]
            for c in range(1, chips):
                total = total + self.recv[c]
            self.near().wait_send()
            for k in range(1, chips):
                self.wide(k).wait_send()
            return total

    def lines(table, phase):
        return [Line(table.at[c], line_sems.at[phase, c], nf) for c in range(chunks)]

    def gather_total(total, table, phase):
        gathers = lines(table, phase)
        for c in range(chunks):
            for i in range(part):
                table[c, f, :, lanes(i)] = total[c * part + i].astype(BF16)
            gathers[c].start()
        return gathers

    def place(target, value, c):
        for i in range(part):
            target[me, c * part + i] = value[:, lanes(i)]

    first = Gather(tab1, 0)
    for c in range(chunks):
        for rb in range(c * part, (c + 1) * part):
            tab1[me, rb] = features[:, lanes(rb)]
        first.start(c)
    w_in_t[...] = w_in[...].T
    w_mid_t[...] = w_mid[...].T
    first.aggregate(acc1, prod1, win1)
    gathers = gather_total(acc1, line1, 0)
    follow = Gather(tab2, 1)
    own_in = own_rows(w_in_t)
    for c in range(chunks):
        gathers[c].finish()
        if in_part % 16 == 0:
            pre = dot(own_in, line1[c].reshape(nf * in_part, part * blk))
        else:
            pre = dot(own_in[:, 0:in_part], line1[c, 0])
            for g in range(1, nf):
                pre += dot(own_in[:, g * in_part : (g + 1) * in_part], line1[c, g])
        pre1[c] = pre
        place(tab2, elu(pre).astype(BF16), c)
        follow.start(c)
    for g in gathers:
        g.drain()

    follow.aggregate(acc, prod, back)
    gathers = gather_total(acc, line2, 1)
    follow = Gather(tab3, 2)
    for c in range(chunks):
        gathers[c].finish()
        pre = dot(own_rows(w_mid_t), line2[c].reshape(hidden, part * blk))
        pre2[c] = pre
        place(tab3, elu(pre).astype(BF16), c)
        follow.start(c)
    for g in gathers:
        g.drain()

    follow.aggregate(acc, prod, back)
    gathers = gather_total(acc, line3, 2)
    loss_part = 0.0
    count_part = 0.0
    grad_part = None
    for c in range(chunks):
        gathers[c].finish()
        span = slice(c * part * blk, (c + 1) * part * blk)
        logits = lax.dot_general(
            w_out[...], line3[c].reshape(hidden, part * blk), (((0,), (0,)), ((), ())),
            preferred_element_type=F32,
        )
        rows = lax.broadcasted_iota(jnp.int32, logits.shape, 0)
        log_total = jnp.log(jnp.sum(jnp.exp(logits), axis=0, keepdims=True))
        one_hot = jnp.where(rows == labels[:, span], 1.0, 0.0)
        picked = jnp.sum(one_hot * logits, axis=0, keepdims=True)
        weighting = mask[:, span].astype(F32)
        loss_part += jnp.sum(weighting * (log_total - picked))
        count_part += jnp.sum(weighting)
        grads = (weighting * (jnp.exp(logits - log_total) - one_hot)).astype(BF16)
        third = dot(own_rows(w_out), grads).astype(BF16)
        for i in range(part):
            back[c * part + i] = third[:, lanes(i)]
        term = dot_nt(line3[c, f], grads)
        grad_part = term if grad_part is None else grad_part + term
    for g in gathers:
        g.drain()
    go_mine[...] = jnp.zeros_like(go_mine)
    go_mine[0:hp, 0:classes] = grad_part
    stat_rows = lax.broadcasted_iota(jnp.int32, (8, go_mine.shape[1]), 0)
    go_mine[hp : hp + 8, :] = jnp.where(stat_rows == 0, loss_part, count_part)
    go_sum = Total(0, go_mine, go_part, go_pair, go_recv)
    go_sum.near().start()

    gathers = lines(line4, 3)

    def ready_second(c, rb, total):
        if rb is None:
            gathers[c].start()
        else:
            i = rb - c * part
            slope = elu_slope(pre2[c, :, lanes(i)])
            line4[c, f, :, lanes(i)] = (total * slope).astype(BF16)

    spread(0, acc, ready_second)
    go_sum.spread_pair()
    grad_part = None
    for c in range(chunks):
        gathers[c].finish()
        gate = line4[c].reshape(hidden, part * blk)
        second = dot(own_rows(w_mid), gate).astype(BF16)
        for i in range(part):
            back[c * part + i] = second[:, lanes(i)]
        term = dot_nt(line2[c, f], gate)
        grad_part = term if grad_part is None else grad_part + term
    for g in gathers:
        g.drain()
    gm_mine[...] = grad_part
    gm_sum = Total(1, gm_mine, gm_part, gm_pair, gm_recv)
    gm_sum.near().start()

    def ready_first(c, rb, total):
        if rb is not None:
            i = rb - c * part
            slope = elu_slope(pre1[c, :, lanes(i)])
            gate1[c, :, lanes(i)] = (total * slope).astype(BF16)

    spread(1, acc, ready_first)
    gm_sum.spread_pair()
    for g in range(nf):
        term = dot_nt(line1[0, g], gate1[0])
        for c in range(1, chunks):
            term += dot_nt(line1[c, g], gate1[c])
        gi_own[g] = term

    def swap(k):
        target = lax.rem(f + k, nf)
        return pltpu.make_async_remote_copy(
            src_ref=gi_own.at[target], dst_ref=gi_swap.at[f],
            send_sem=swap_sems.at[0, k], recv_sem=swap_sems.at[1, k],
            device_id={"feat": target}, device_id_type=MESH,
        )

    for k in range(1, nf):
        swap(k).start()
    gi_swap[f] = gi_own[f]
    total = go_sum.result()
    gout_out[...] = total[0:hp, 0:classes]
    loss_out[...] = total[hp : hp + 1, 0:1] / jnp.maximum(total[hp + 1 : hp + 2, 0:1], 1.0)
    gmid_out[...] = gm_sum.result()
    for k in range(1, nf):
        slot = gi_swap.at[lax.rem(f - k + nf, nf)]
        pltpu.make_async_copy(slot, slot, swap_sems.at[1, k]).wait()
    for g in range(nf):
        gi_mine[:, g * hp : (g + 1) * hp] = gi_swap[g]
    gi_sum = Total(2, gi_mine, gi_part, gi_pair, gi_recv)
    gi_sum.near().start()
    gi_sum.spread_pair()
    for k in range(1, nf):
        swap(k).wait_send()
    gin_out[...] = gi_sum.result()


def round_up(value, step):
    return (value + step - 1) // step * step


def shards(
    features, weight_in, weight_mid, weight_out, block_values,
    block_dst, block_src, block_count, labels, train_mask,
):
    n = lax.axis_size("blk")
    nf = lax.axis_size("feat")
    in_part, nodes = features.shape
    hidden, classes = weight_out.shape
    hp = hidden // nf
    slots, blk = block_values.shape[2], block_values.shape[-1]
    rb_count = nodes // blk
    wide = round_up(classes, 128)
    chips = n // 2
    chunks = 2 if rb_count % 2 == 0 else 1
    span = nodes // chunks

    vmem = pl.BlockSpec(memory_space=pltpu.VMEM)
    smem = pl.BlockSpec(memory_space=pltpu.SMEM)

    def sums(rows, width):
        return [pltpu.VMEM((rows, width), F32)] * 3 + [pltpu.VMEM((chips, rows, width), F32)]

    tab = pltpu.VMEM((n, rb_count, hp, blk), BF16)
    line = pltpu.VMEM((chunks, nf, hp, span), BF16)
    stage = pltpu.VMEM((2, chips, rb_count, hp, blk), BF16)
    loss, gin, gmid, gout = pl.pallas_call(
        functools.partial(step_kernel, n, nf, chunks, slots),
        out_shape=(
            jax.ShapeDtypeStruct((1, 1), F32),
            jax.ShapeDtypeStruct((in_part, hidden), F32),
            jax.ShapeDtypeStruct((hp, hidden), F32),
            jax.ShapeDtypeStruct((hp, classes), F32),
        ),
        in_specs=[vmem] * 5 + [smem] * 3 + [vmem] * 2,
        out_specs=(vmem,) * 4,
        scratch_shapes=[
            pltpu.VMEM((n, rb_count, in_part, blk), BF16), tab, tab,
            pltpu.VMEM((chunks, nf, in_part, span), BF16), line, line, line,
            pltpu.VMEM((rb_count, hp, blk), BF16),
            pltpu.VMEM((rb_count, hp, blk), F32),
            pltpu.VMEM((slots, hp, blk), F32),
            pltpu.VMEM((rb_count, in_part, blk), BF16),
            pltpu.VMEM((rb_count, in_part, blk), F32),
            pltpu.VMEM((slots, in_part, blk), F32),
            pltpu.VMEM((chunks, hp, span), F32), pltpu.VMEM((chunks, hp, span), F32),
            pltpu.VMEM((hidden, weight_in.shape[0]), BF16),
            pltpu.VMEM((hidden, hidden), BF16),
            pltpu.VMEM((chunks, hp, span), BF16),
            stage, stage, stage, stage,
            *sums(hp + 8, wide), *sums(hp, hidden), *sums(in_part, hidden),
            pltpu.VMEM((nf, in_part, hp), F32), pltpu.VMEM((nf, in_part, hp), F32),
            pltpu.SemaphoreType.DMA((3, 4, chips, chunks)),
            pltpu.SemaphoreType.DMA((4, chunks, 4, nf + 1)),
            pltpu.SemaphoreType.DMA((2, 4, chips, chunks)),
            pltpu.SemaphoreType.DMA((3, 2, chips)),
            pltpu.SemaphoreType.DMA((2, nf)),
        ],
        compiler_params=pltpu.CompilerParams(
            collective_id=0, has_side_effects=True, vmem_limit_bytes=56 * 1024 * 1024
        ),
        name="step",
    )(
        features, weight_in, weight_mid, weight_out, block_values,
        block_dst, block_src, block_count, labels.reshape(1, -1), train_mask.reshape(1, -1),
    )
    return loss.reshape(()), gin, gmid, gout


def solution(mesh):
    placed = (
        P("feat", "blk"), P(), P(), P(), P("blk", None, None, None, None),
        P("blk", None, None), P("blk", None, None), P("blk", None), P("blk"), P("blk"),
    )
    return jax.shard_map(
        shards,
        mesh=mesh,
        in_specs=placed,
        out_specs=(P(), P("feat", None), P("feat", None), P("feat", None)),
        check_vma=False,
    )
```
